32 devices in a mesh: parts: 2 (over y), ctx: 4 (over z), head: 2 (over x), fsdp: 2 (over core).
Axes of the slice: x: 2, y: 2, z: 4, core: 2. Of those that a mesh axis runs over, the one named last changes fastest.
Arguments:
- mixer_input_channels: bfloat16 [4096, 4096], P(('parts', 'ctx'), ('head', 'fsdp')), parts along dimension 0, may hold values from -6 to 6
- gate_channels: bfloat16 [4096, 4096], P(('parts', 'ctx'), ('head', 'fsdp')), parts along dimension 0, may hold values from -6 to 6
- input_group_maps: bfloat16 [4096, 1024], P(('parts', 'ctx'), ('head', 'fsdp')), parts along dimension 0, may hold values from -6 to 6
- output_group_maps: bfloat16 [4096, 1024], P(('parts', 'ctx'), ('head', 'fsdp')), parts along dimension 0, may hold values from -6 to 6
- step_size_input: float32 [64, 4096], P(('head', 'fsdp'), ('parts', 'ctx')), parts along dimension 1, may hold values from -4 to 4
- resets: int32 [4096], P(('parts', 'ctx')), parts along dimension 0, may hold values 0 or 1
- head_decay_rate: float32 [64], P(('head', 'fsdp')), may hold values from 2e-07 to 0.035
- step_size_bias: float32 [64], P(('head', 'fsdp')), may hold values from -1 to 1
- skip: float32 [64], P(('head', 'fsdp')), may hold values from 0.5 to 1.5
- gated_norm_gain: float32 [4096], P(('head', 'fsdp')), may hold values from 0.5 to 1.5
- adapter_down_map: bfloat16 [4096, 64], P(('head', 'fsdp')), may hold values from -0.09375 to 0.09375
- adapter_up_map: bfloat16 [64, 4096], P(None, ('head', 'fsdp')), may hold values from -0.75 to 0.75
- frozen_mixed_gradient: bfloat16 [4096, 4096], P(('parts', 'ctx'), ('head', 'fsdp')), parts along dimension 0, may hold values from -6 to 6
- layer_output_gradient: bfloat16 [4096, 4096], P(('parts', 'ctx'), ('head', 'fsdp')), parts along dimension 0, may hold values from -6 to 6
Outputs:
- mixed: bfloat16 [4096, 4096], P(('parts', 'ctx'), ('head', 'fsdp')), parts along dimension 0
- adapter_output: bfloat16 [4096, 4096], P(('parts', 'ctx'), ('head', 'fsdp')), parts along dimension 0
- mixer_input_gradient: bfloat16 [4096, 4096], P(('parts', 'ctx'), ('head', 'fsdp')), parts along dimension 0
- gate_input_gradient: bfloat16 [4096, 4096], P(('parts', 'ctx'), ('head', 'fsdp')), parts along dimension 0
- input_maps_gradient: bfloat16 [4096, 1024], P(('parts', 'ctx'), ('head', 'fsdp')), parts along dimension 0
- output_maps_gradient: bfloat16 [4096, 1024], P(('parts', 'ctx'), ('head', 'fsdp')), parts along dimension 0
- step_size_gradient: float32 [64, 4096], P(('head', 'fsdp'), ('parts', 'ctx')), parts along dimension 1
- adapter_down_gradient: float32 [8192, 64], P(('parts', 'head', 'fsdp')), parts along dimension 0
- adapter_up_gradient: float32 [128, 4096], P('parts', ('head', 'fsdp')), parts along dimension 0
The draws below stay inside these ranges and needn't reach their ends.
There are 2 independent parts, one for each index of `parts`. The reference program is written for one: setup_inputs(seed, part) draws one part's arguments, and reference() takes and returns one part's arrays. A program takes and returns all parts, laid end to end along the dimension named above; an argument that names none is the same for every part. Nothing has to cross between parts.
All inputs are finite; a program needn't handle non-finite values. No bound on the sum of `resets` on one device may be relied on, other than what follows from the above.
Results may differ from the reference program's by a relative error of at most 0.0057.
Values sent between devices are 32-bit elements; how exact they have to be, the bound alone decides.
A program may use at most 128 MiB of HBM per device.

```python
import math
from functools import partial
import jax
import jax.numpy as jnp
from jax import lax

MODEL_WIDTH = 4096
MIXER_HEADS = 64
HEAD_CHANNELS = 64
STATE = 128
GROUPS = 8
ADAPTER_RANK = 64
SPAN = 256
LENGTH = 2048


def draw_head_decay_rate(key, part):
    lower = math.log(4e-07)
    upper = math.log(0.035)
    return jnp.exp(jax.random.uniform(key, (MIXER_HEADS,), jnp.float32, lower, upper))


def plant(result, rng, smallest, largest):
    longest = result.shape.index(max(result.shape))
    spots = []
    for shift in (0, 1):
        where = [jax.random.randint(jax.random.fold_in(rng, axis), (), 0, length) for axis, length in enumerate(result.shape)]
        where[longest] = (where[longest] + shift) % result.shape[longest]
        spots.append(tuple(where))
    return result.at[spots[0]].set(smallest).at[spots[1]].set(largest)


def steps_of(rng, extent, shards, smallest, largest):
    def one(axis_at, parts):
        draws = jax.random.uniform(jax.random.fold_in(jax.random.fold_in(rng, 6), axis_at), (parts,), jnp.float32, smallest / len(shards), largest / len(shards))
        return jnp.repeat(jnp.exp(draws), extent[axis_at] // parts).reshape((-1,) + (1,) * (len(extent) - axis_at - 1))

    level = one(*shards[0])
    for cut in shards[1:]:
        level = level * one(*cut)
    return level


def bell_draw(own_key, dims, deviation, limit, split=(), kind=jnp.bfloat16):
    result = deviation * jax.random.normal(own_key, dims, jnp.float32)
    if split:
        result = result * steps_of(own_key, dims, split, -0.22, 0.18)
    return jnp.clip(result, -limit, limit).astype(kind)


def setup_inputs(seed: int = 0, part: int = 0) -> dict:
    streams_of = jax.random.split(jax.random.key(seed), 15)
    own_keys = jax.random.split(jax.random.fold_in(streams_of[14], part), 15)
    return {
        "mixer_input_channels": bell_draw(own_keys[0], (LENGTH, MIXER_HEADS * HEAD_CHANNELS), 1.0, 6.0, ((0, 4), (1, 4))),
        "gate_channels": bell_draw(own_keys[1], (LENGTH, MIXER_HEADS * HEAD_CHANNELS), 1.0, 6.0, ((0, 4), (1, 4))),
        "input_group_maps": bell_draw(own_keys[2], (LENGTH, GROUPS * STATE), 1.0, 6.0, ((0, 4), (1, 4))),
        "output_group_maps": bell_draw(own_keys[3], (LENGTH, GROUPS * STATE), 1.0, 6.0, ((0, 4), (1, 4))),
        "step_size_input": bell_draw(own_keys[4], (MIXER_HEADS, LENGTH), 1.0, 4.0, ((0, 4), (1, 4)), jnp.float32),
        "resets": plant((jax.random.randint(own_keys[5], (LENGTH,), 0, 4096) < 1).astype(jnp.int32), jax.random.fold_in(own_keys[5], 1), 0, 1),
        "head_decay_rate": draw_head_decay_rate(jax.random.fold_in(streams_of[14], 71), part),
        "step_size_bias": jnp.clip(jax.random.uniform(streams_of[7], (MIXER_HEADS,), jnp.float32, -1.0, 1.0) * steps_of(streams_of[7], (MIXER_HEADS,), ((0, 4),), -0.4, 0.0), -1.0, 1.0),
        "skip": jnp.clip(0.5 + 1.0 * jax.random.uniform(streams_of[8], (MIXER_HEADS,), jnp.float32) ** steps_of(streams_of[8], (MIXER_HEADS,), ((0, 4),), -0.2, 0.2), 0.5, 1.5),
        "gated_norm_gain": jnp.clip(1.0 + 0.1 * jax.random.normal(streams_of[9], (MIXER_HEADS * HEAD_CHANNELS,), jnp.float32), 0.5, 1.5),
        "adapter_down_map": bell_draw(streams_of[10], (MIXER_HEADS * HEAD_CHANNELS, ADAPTER_RANK), (MIXER_HEADS * HEAD_CHANNELS) ** -0.5, 0.09375, ((0, 4),)),
        "adapter_up_map": bell_draw(streams_of[11], (ADAPTER_RANK, MODEL_WIDTH), ADAPTER_RANK ** -0.5, 0.75, ((1, 4),)),
        "frozen_mixed_gradient": bell_draw(own_keys[12], (LENGTH, MIXER_HEADS * HEAD_CHANNELS), 1.0, 6.0, ((0, 4), (1, 4))),
        "layer_output_gradient": bell_draw(own_keys[13], (LENGTH, MODEL_WIDTH), 1.0, 6.0, ((0, 4), (1, 4))),
    }


eps = 1e-05
adapter_scale = 2.0
highest = lax.Precision.HIGHEST

def span_step(rates, state, pieces):
    x_part, b_part, c_part, dt_part, r_part = pieces
    width = r_part.shape[0]
    per_group = x_part.shape[1] // b_part.shape[1]
    cum_log = jnp.cumsum(-rates[:, None] * dt_part, axis=1)
    reset_ids = jnp.cumsum(r_part)
    places = jnp.arange(width)
    same_mask = (reset_ids[:, None] == reset_ids[None, :]) & (places[:, None] >= places[None, :])
    log_gap = cum_log[:, :, None] - cum_log[:, None, :]
    damping = jnp.where(same_mask[None], jnp.exp(jnp.where(same_mask[None], log_gap, 0.0)), 0.0)
    scores = jnp.repeat(jnp.einsum('rgn,sgn->grs', c_part, b_part, precision=highest), per_group, axis=0)
    b_heads = jnp.repeat(b_part, per_group, axis=1)
    c_heads = jnp.repeat(c_part, per_group, axis=1)
    weights = damping * scores * dt_part[:, None, :]
    y_loc = jnp.einsum('hrs,shp->rhp', weights, x_part, precision=highest)
    from_start = jnp.exp(cum_log) * (reset_ids == 0)[None, :]
    y_carry = jnp.einsum('rhn,hpn->rhp', c_heads, state, precision=highest) * from_start.T[:, :, None]
    to_end = jnp.exp(cum_log[:, -1:] - cum_log) * (reset_ids == reset_ids[-1])[None, :]
    total = jnp.exp(cum_log[:, -1]) * (reset_ids[-1] == 0)
    scaled = x_part * (to_end * dt_part).T[:, :, None]
    new_state = total[:, None, None] * state + jnp.einsum('shp,shn->hpn', scaled, b_heads, precision=highest)
    return (new_state, y_loc + y_carry)

def mixer(mixer_input_channels, gate_channels, input_group_maps, output_group_maps, step_size_input, resets, head_decay_rate, step_size_bias, skip, gated_norm_gain):
    seq_len, channels = mixer_input_channels.shape
    head_count = step_size_input.shape[0]
    head_dim = channels // head_count
    groups = input_group_maps.shape[1] // STATE
    per_group = head_count // groups
    spans = seq_len // SPAN
    inputs = mixer_input_channels.astype(jnp.float32).reshape(seq_len, head_count, head_dim)
    b_group = input_group_maps.astype(jnp.float32).reshape(spans, SPAN, groups, STATE)
    c_group = output_group_maps.astype(jnp.float32).reshape(spans, SPAN, groups, STATE)
    dt_full = jax.nn.softplus(step_size_input + step_size_bias[:, None])
    pieces = (inputs.reshape(spans, SPAN, head_count, head_dim), b_group, c_group, dt_full.reshape(head_count, spans, SPAN).transpose(1, 0, 2), resets.reshape(spans, SPAN))
    start = jnp.zeros((head_count, head_dim, STATE), jnp.float32)
    stepper = jax.checkpoint(partial(span_step, head_decay_rate))
    final, outputs = lax.scan(stepper, start, pieces)
    y_full = outputs.reshape(seq_len, head_count, head_dim) + skip[None, :, None] * inputs
    gates_in = gate_channels.astype(jnp.float32).reshape(seq_len, head_count, head_dim)
    gated = y_full * jax.nn.silu(gates_in)
    grouped = gated.reshape(seq_len, groups, per_group * head_dim)
    normed = grouped * lax.rsqrt(lax.optimization_barrier(jnp.mean(grouped * grouped, axis=-1, keepdims=True)) + eps)
    return normed.reshape(seq_len, channels) * gated_norm_gain[None, :]

def reference(mixer_input_channels, gate_channels, input_group_maps, output_group_maps, step_size_input, resets, head_decay_rate, step_size_bias, skip, gated_norm_gain, adapter_down_map, adapter_up_map, frozen_mixed_gradient, layer_output_gradient):

    def forward(x_arg, z_arg, b_arg, c_arg, dt_arg):
        return mixer(x_arg, z_arg, b_arg, c_arg, dt_arg, resets, head_decay_rate, step_size_bias, skip, gated_norm_gain)
    scaled_out, pullback = jax.vjp(forward, mixer_input_channels, gate_channels, input_group_maps, output_group_maps, step_size_input)
    mixed = scaled_out.astype(jnp.bfloat16)
    low_rank_projected = (adapter_scale * jnp.dot(mixed, adapter_down_map, preferred_element_type=jnp.float32)).astype(jnp.bfloat16)
    adapter_output = jnp.dot(low_rank_projected, adapter_up_map, preferred_element_type=jnp.float32).astype(jnp.bfloat16)
    low_rank_gradient = (adapter_scale * jnp.dot(layer_output_gradient, adapter_up_map.T, preferred_element_type=jnp.float32)).astype(jnp.bfloat16)
    mixed_gradient = frozen_mixed_gradient.astype(jnp.float32) + jnp.dot(low_rank_gradient, adapter_down_map.T, preferred_element_type=jnp.float32)
    mixer_input_gradient, gate_input_gradient, input_maps_gradient, output_maps_gradient, step_size_gradient = pullback(mixed_gradient)
    adapter_down_gradient = jnp.dot(mixed.T, low_rank_gradient, preferred_element_type=jnp.float32)
    adapter_up_gradient = jnp.dot(low_rank_projected.T, layer_output_gradient, preferred_element_type=jnp.float32)
    return (mixed, adapter_output, mixer_input_gradient.astype(jnp.bfloat16), gate_input_gradient.astype(jnp.bfloat16), input_maps_gradient.astype(jnp.bfloat16), output_maps_gradient.astype(jnp.bfloat16), step_size_gradient.astype(jnp.float32), adapter_down_gradient, adapter_up_gradient)
```

```python
import jax
import jax.numpy as jnp
from jax import lax
from jax.experimental import pallas as pl
from jax.experimental.pallas import tpu as pltpu
from jax.sharding import PartitionSpec as P

STATE = 128
LANES = 128
eps = 1e-05
adapter_scale = 2.0
highest = lax.Precision.HIGHEST
f32 = jnp.float32
bf16 = jnp.bfloat16


def nn(a, b):
    return lax.dot_general(a, b, (((1,), (0,)), ((), ())), preferred_element_type=f32)


def nt(a, b):
    return lax.dot_general(a, b, (((1,), (1,)), ((), ())), preferred_element_type=f32)


def tn(a, b):
    return lax.dot_general(a, b, (((0,), (0,)), ((), ())), preferred_element_type=f32)


def split(a):
    hi = a.astype(bf16)
    return hi, (a - hi.astype(f32)).astype(bf16)


def iota(shape, dim):
    return lax.broadcasted_iota(jnp.int32, shape, dim)


def expand(cols, group, per_group, width):
    pick = (iota((LANES, width), 0) == group * per_group + iota((LANES, width), 1) // (width // per_group))
    pick = jnp.where(pick, 1.0, 0.0).astype(bf16)
    hi, lo = split(cols)
    return nn(hi, pick) + nn(lo, pick)


def headsum(values, group, per_group):
    width = values.shape[1]
    pick = (iota((width, LANES), 1) == group * per_group + iota((width, LANES), 0) // (width // per_group))
    pick = jnp.where(pick, 1.0, 0.0).astype(bf16)
    hi, lo = split(values)
    return nn(hi, pick) + nn(lo, pick)


def score_mask(rid_col, rid_row):
    n = rid_col.shape[0]
    return (rid_col == rid_row) & (iota((n, n), 0) >= iota((n, n), 1))


def scan_kernel(x_ref, b_ref, dtin_ref, bias_ref, rate_ref, resets_ref,
                e_ref, einv_ref, dt_ref, rc_ref, rr_ref, em_ref, state_ref):
    rows = x_ref.shape[0]
    heads = dtin_ref.shape[0]
    groups = b_ref.shape[1] // STATE
    per_group = heads // groups
    width = x_ref.shape[1] // groups
    v = dtin_ref[...] + bias_ref[...]
    dt = jnp.maximum(v, 0.0) + jnp.log1p(jnp.exp(-jnp.abs(v)))
    log_step = -rate_ref[...] * dt
    marks = jnp.broadcast_to(resets_ref[...].astype(f32), (8, rows))
    stack = jnp.concatenate([log_step, marks, jnp.zeros((LANES - heads - 8, rows), f32)], axis=0)
    dt_cols = jnp.concatenate([dt, jnp.zeros((LANES - heads, rows), f32)], axis=0).T
    tri = jnp.where(iota((rows, rows), 0) >= iota((rows, rows), 1), 1.0, 0.0)
    cum = lax.dot_general(tri, stack.T, (((1,), (0,)), ((), ())), precision=highest, preferred_element_type=f32)
    cum_rows = cum.T
    rid_col = cum[:, heads : heads + 1]
    rid_row = cum_rows[heads : heads + 1, :]
    rid_last = cum[rows - 1 : rows, heads : heads + 1]
    cum_heads = jnp.where(iota((rows, LANES), 1) < heads, cum, 0.0)
    mid = 0.5 * cum_heads[rows - 1 : rows, :]
    e_ref[...] = jnp.exp(cum_heads - mid)
    einv = jnp.exp(mid - cum_heads)
    einv_ref[...] = einv
    dt_ref[...] = dt_cols
    f_cols = dt_cols * einv
    rc_ref[...] = jnp.broadcast_to(rid_col, rc_ref.shape)
    rr_ref[...] = jnp.broadcast_to(rid_row, rr_ref.shape)
    ends = rid_col == rid_last
    unbroken = jnp.where(rid_last == 0, 1.0, 0.0)
    em_cols = jnp.broadcast_to(jnp.exp(mid), (8, LANES))
    for g in range(groups):
        cols = slice(g * width, (g + 1) * width)
        em = expand(em_cols, g, per_group, width)
        xd = (x_ref[:, cols].astype(f32) * expand(f_cols, g, per_group, width)).astype(bf16)
        b_end = jnp.where(ends, b_ref[:, g * STATE : (g + 1) * STATE], 0.0).astype(bf16)
        em_ref[:, cols] = em
        state_ref[:STATE, cols] = em[:1] * tn(b_end, xd)
        state_ref[STATE:, cols] = em * em * unbroken


def forward_kernel(ctx, heads, place_ref, x_ref, z_ref, b_ref, c_ref, gx_ref, e_ref, einv_ref, dt_ref, rc_ref,
                   rr_ref, em_ref, skip_ref, gain_ref, down_ref, gu_ref, gathered_ref,
                   mixed_ref, dz_ref, gy_ref, gd_ref, sin_ref, ginj_ref, pn_ref, k_ref, ddown_ref, u_ref):
    rows = x_ref.shape[0]
    groups = b_ref.shape[1] // STATE
    width = x_ref.shape[1] // groups
    per_group = heads // groups
    place = place_ref[0]

    sin_ref[...] = jnp.zeros_like(sin_ref)

    def fold(j, _):
        sin_ref[...] = gathered_ref[j, STATE : STATE + 1, :] * sin_ref[...] + gathered_ref[j, :STATE, :]
        return 0

    lax.fori_loop(0, place, fold, 0)
    mask = score_mask(rc_ref[:, :1], rr_ref[:1, :])
    fresh = rc_ref[:, :1] == 0
    f_cols = dt_ref[...] * einv_ref[...]
    gu = gu_ref[...]
    u = jnp.zeros(u_ref.shape, f32)
    pn = jnp.zeros(pn_ref.shape, f32)
    kk = jnp.zeros((8, LANES), f32)
    for g in range(groups):
        cols = slice(g * width, (g + 1) * width)
        narrow = slice(g * STATE, (g + 1) * STATE)
        x = x_ref[:, cols].astype(f32)
        ex = expand(e_ref[...], g, per_group, width)
        xd = (x * expand(f_cols, g, per_group, width)).astype(bf16)
        c = c_ref[:, narrow]
        a = jnp.where(mask, nt(c, b_ref[:, narrow]), 0.0).astype(bf16)
        c0 = jnp.where(fresh, c, 0.0).astype(bf16)
        em = em_ref[:1, cols]
        s = (em * sin_ref[:, cols]).astype(bf16)
        inner = nn(a, xd) + nn(c0, s)
        y = ex * inner + skip_ref[:, cols] * x
        z = z_ref[:, cols].astype(f32)
        sig = 1.0 / (1.0 + jnp.exp(-z))
        act = z * sig
        gated = y * act
        inv = lax.rsqrt(jnp.mean(gated * gated, axis=-1, keepdims=True) + eps)
        normed = gated * inv
        gain = gain_ref[:, cols]
        mixed = (normed * gain).astype(bf16)
        mixed_ref[:, cols] = mixed
        down = down_ref[cols, :]
        u = u + nn(mixed, down)
        ddown_ref[cols, :] = tn(mixed, gu)
        gn = (gx_ref[:, cols].astype(f32) + nt(gu, down)) * gain
        gg = inv * (gn - normed * jnp.mean(gn * normed, axis=-1, keepdims=True))
        gy = gg * act
        dz_ref[:, cols] = (gg * y * sig * (1.0 + z * (1.0 - sig))).astype(bf16)
        gy_ref[:, cols] = gy
        gd = (gy * ex).astype(bf16)
        gd_ref[:, cols] = gd
        inj = tn(c0, gd)
        ginj_ref[:STATE, cols] = em * inj
        pn = pn + headsum(gd.astype(f32) * inner, g, per_group)
        kk = kk + headsum(jnp.broadcast_to(jnp.sum(s.astype(f32) * inj, axis=0, keepdims=True), (8, width)), g, per_group)
    ginj_ref[STATE:, :] = gathered_ref[place, STATE:, :]
    u_ref[...] = u
    pn_ref[...] = pn
    k_ref[...] = kk


def backward_kernel(ctx, heads, place_ref, x_ref, b_ref, c_ref, e_ref, einv_ref, dt_ref, rc_ref, rr_ref, em_ref,
                    skip_ref, rate_ref, gy_ref, gd_ref, sin_ref, pn_ref, k_ref, gathered_ref,
                    dx_ref, db_ref, dc_ref, dstep_ref, gin_ref):
    rows = x_ref.shape[0]
    groups = b_ref.shape[1] // STATE
    width = x_ref.shape[1] // groups
    per_group = heads // groups
    place = place_ref[0]

    gin_ref[...] = jnp.zeros_like(gin_ref)

    def fold(i, _):
        j = ctx - 1 - i
        gin_ref[...] = gathered_ref[j, STATE : STATE + 1, :] * gin_ref[...] + gathered_ref[j, :STATE, :]
        return 0

    lax.fori_loop(0, ctx - 1 - place, fold, 0)
    decay_row = gathered_ref[place, STATE : STATE + 1, :]
    mask = score_mask(rc_ref[:, :1], rr_ref[:1, :])
    fresh = rc_ref[:, :1] == 0
    ends = rc_ref[:, :1] == rc_ref[rows - 1 : rows, :1]
    f_cols = dt_ref[...] * einv_ref[...]
    net = -pn_ref[...]
    step = jnp.zeros(pn_ref.shape, f32)
    kk = k_ref[...]
    for g in range(groups):
        cols = slice(g * width, (g + 1) * width)
        narrow = slice(g * STATE, (g + 1) * STATE)
        x = x_ref[:, cols].astype(f32)
        fx = expand(f_cols, g, per_group, width)
        xd = (x * fx).astype(bf16)
        gd = gd_ref[:, cols]
        b = b_ref[:, narrow]
        c = c_ref[:, narrow]
        a = jnp.where(mask, nt(c, b), 0.0).astype(bf16)
        b_end = jnp.where(ends, b, 0.0).astype(bf16)
        em = em_ref[:1, cols]
        sin = sin_ref[:, cols]
        gin = gin_ref[:, cols]
        s = (em * sin).astype(bf16)
        ge = (em * gin).astype(bf16)
        v = tn(a, gd) + nn(b_end, ge)
        dx_ref[:, cols] = (fx * v + skip_ref[:, cols] * gy_ref[:, cols]).astype(bf16)
        pair = jnp.where(mask, nt(gd, xd), 0.0).astype(bf16)
        dc_ref[:, narrow] = (nn(pair, b) + jnp.where(fresh, nt(gd, s), 0.0)).astype(bf16)
        db_ref[:, narrow] = (tn(pair, c) + jnp.where(ends, nt(xd, ge), 0.0)).astype(bf16)
        net = net + headsum(xd.astype(f32) * v, g, per_group)
        step = step + headsum(x * v, g, per_group)
        through = decay_row[:, cols] * jnp.sum(sin * gin, axis=0, keepdims=True)
        kk = kk + headsum(jnp.broadcast_to(through, (8, width)), g, per_group)
    before = jnp.where(iota((rows, rows), 0) > iota((rows, rows), 1), 1.0, 0.0)
    glog = lax.dot_general(before, net, (((1,), (0,)), ((), ())), precision=highest, preferred_element_type=f32) + kk[:1]
    gdt = einv_ref[...] * step - rate_ref[...] * glog
    out = gdt * (1.0 - jnp.exp(-dt_ref[...]))
    dstep_ref[...] = out.T[: dstep_ref.shape[0], :]


def vm():
    return pl.BlockSpec(memory_space=pltpu.VMEM)


def call(kernel, name, outs, args, scalars=0):
    specs = [pl.BlockSpec(memory_space=pltpu.SMEM)] * scalars + [vm()] * (len(args) - scalars)
    return pl.pallas_call(
        kernel,
        name=name,
        out_shape=[jax.ShapeDtypeStruct(s, d) for s, d in outs],
        in_specs=specs,
        out_specs=[vm()] * len(outs),
        compiler_params=pltpu.CompilerParams(vmem_limit_bytes=56 << 20),
    )(*args)


def per_device(x, z, b, c, dtin, resets, rate, bias, skip, gain, down, up, gx, gout):
    rows, channels = x.shape
    heads = dtin.shape[0]
    rank = down.shape[1]
    ctx = lax.axis_size("ctx")
    place = lax.axis_index("ctx").astype(jnp.int32).reshape(1)
    head_dim = channels // heads
    wide = STATE + 8
    gu_part = nt(gout, up)
    gu = (adapter_scale * lax.psum(gu_part, ("head", "fsdp"))).astype(bf16)
    skip_row = jnp.repeat(skip, head_dim)[None, :]
    gain_row = gain[None, :]
    rate_row = jnp.pad(rate, (0, LANES - heads))[None, :]
    e, einv, dt, rc, rr, em, state = call(
        scan_kernel, "scan",
        [((rows, LANES), f32)] * 4 + [((8, rows), f32), ((8, channels), f32), ((wide, channels), f32)],
        (x, b, dtin, bias[:, None], rate[:, None], resets[None, :]),
    )
    gathered = lax.all_gather(state, "ctx")
    mixed, dz, gy, gd, sin, ginj, pn, kk, ddown, u_part = call(
        lambda *r: forward_kernel(ctx, heads, *r), "forward",
        [((rows, channels), bf16), ((rows, channels), bf16), ((rows, channels), f32), ((rows, channels), bf16),
         ((STATE, channels), f32), ((wide, channels), f32), ((rows, LANES), f32), ((8, LANES), f32),
         ((channels, rank), f32), ((rows, rank), f32)],
        (place, x, z, b, c, gx, e, einv, dt, rc, rr, em, skip_row, gain_row, down, gu, gathered), 1,
    )
    back = lax.all_gather(ginj, "ctx")
    u = (adapter_scale * lax.psum(u_part, ("head", "fsdp"))).astype(bf16)
    adapter_output = nn(u, up).astype(bf16)
    dup = tn(u, gout)
    ddown, dup = lax.psum((ddown, dup), "ctx")
    dx, db, dc, dstep, _ = call(
        lambda *r: backward_kernel(ctx, heads, *r), "backward",
        [((rows, channels), bf16), (b.shape, bf16), (c.shape, bf16), ((heads, rows), f32), ((STATE, channels), f32)],
        (place, x, b, c, e, einv, dt, rc, rr, em, skip_row, rate_row, gy, gd, sin, pn, kk, back), 1,
    )
    return mixed, adapter_output, dx, dz, db, dc, dstep, ddown, dup


def solution(mesh):
    wide = P(("parts", "ctx"), ("head", "fsdp"))
    steps = P(("head", "fsdp"), ("parts", "ctx"))
    over_heads = P(("head", "fsdp"))
    in_specs = (
        wide, wide, wide, wide, steps, P(("parts", "ctx")), over_heads, over_heads, over_heads, over_heads,
        P(("head", "fsdp"), None), P(None, ("head", "fsdp")), wide, wide,
    )
    out_specs = (
        wide, wide, wide, wide, wide, wide, steps, P(("parts", "head", "fsdp"), None), P("parts", ("head", "fsdp")),
    )
    return jax.shard_map(per_device, mesh=mesh, in_specs=in_specs, out_specs=out_specs, check_vma=False)
```

```python
import jax
import jax.numpy as jnp
from jax import lax
from jax.experimental import pallas as pl
from jax.experimental.pallas import tpu as pltpu
from jax.sharding import PartitionSpec as P

STATE = 128
LANES = 128
eps = 1e-05
adapter_scale = 2.0
highest = lax.Precision.HIGHEST
f32 = jnp.float32
bf16 = jnp.bfloat16


def nn(a, b):
    return lax.dot_general(a, b, (((1,), (0,)), ((), ())), preferred_element_type=f32)


def nt(a, b):
    return lax.dot_general(a, b, (((1,), (1,)), ((), ())), preferred_element_type=f32)


def tn(a, b):
    return lax.dot_general(a, b, (((0,), (0,)), ((), ())), preferred_element_type=f32)


def split(a):
    hi = a.astype(bf16)
    return hi, (a - hi.astype(f32)).astype(bf16)


def iota(shape, dim):
    return lax.broadcasted_iota(jnp.int32, shape, dim)


def expand(cols, group, per_group, width):
    pick = (iota((LANES, width), 0) == group * per_group + iota((LANES, width), 1) // (width // per_group))
    pick = jnp.where(pick, 1.0, 0.0).astype(bf16)
    hi, lo = split(cols)
    return nn(hi, pick) + nn(lo, pick)


def headsum(values, group, per_group):
    width = values.shape[1]
    pick = (iota((width, LANES), 1) == group * per_group + iota((width, LANES), 0) // (width // per_group))
    pick = jnp.where(pick, 1.0, 0.0).astype(bf16)
    hi, lo = split(values)
    return nn(hi, pick) + nn(lo, pick)


def score_mask(rid_col, rid_row):
    n = rid_col.shape[0]
    return (rid_col == rid_row) & (iota((n, n), 0) >= iota((n, n), 1))


def scan_kernel(x_ref, b_ref, dtin_ref, bias_ref, rate_ref, resets_ref,
                e_ref, einv_ref, dt_ref, rc_ref, rr_ref, em_ref, decay_ref, state_ref):
    rows = x_ref.shape[0]
    heads = dtin_ref.shape[0]
    groups = b_ref.shape[1] // STATE
    per_group = heads // groups
    width = x_ref.shape[1] // groups
    v = dtin_ref[...] + bias_ref[...]
    dt = jnp.maximum(v, 0.0) + jnp.log1p(jnp.exp(-jnp.abs(v)))
    log_step = -rate_ref[...] * dt
    marks = jnp.broadcast_to(resets_ref[...].astype(f32), (8, rows))
    stack = jnp.concatenate([log_step, marks, jnp.zeros((LANES - heads - 8, rows), f32)], axis=0)
    dt_cols = jnp.concatenate([dt, jnp.zeros((LANES - heads, rows), f32)], axis=0).T
    tri = jnp.where(iota((rows, rows), 0) >= iota((rows, rows), 1), 1.0, 0.0)
    cum = lax.dot_general(tri, stack.T, (((1,), (0,)), ((), ())), precision=highest, preferred_element_type=f32)
    cum_rows = cum.T
    rid_col = cum[:, heads : heads + 1]
    rid_row = cum_rows[heads : heads + 1, :]
    rid_last = cum[rows - 1 : rows, heads : heads + 1]
    cum_heads = jnp.where(iota((rows, LANES), 1) < heads, cum, 0.0)
    mid = 0.5 * cum_heads[rows - 1 : rows, :]
    e_ref[...] = jnp.exp(cum_heads - mid)
    einv = jnp.exp(mid - cum_heads)
    einv_ref[...] = einv
    dt_ref[...] = dt_cols
    f_cols = dt_cols * einv
    rc_ref[...] = jnp.broadcast_to(rid_col, rc_ref.shape)
    rr_ref[...] = jnp.broadcast_to(rid_row, rr_ref.shape)
    ends = rid_col == rid_last
    unbroken = jnp.where(rid_last == 0, 1.0, 0.0)
    em_cols = jnp.broadcast_to(jnp.exp(mid), (8, LANES))
    for g in range(groups):
        cols = slice(g * width, (g + 1) * width)
        em = expand(em_cols, g, per_group, width)
        xd = (x_ref[:, cols].astype(f32) * expand(f_cols, g, per_group, width)).astype(bf16)
        b_end = jnp.where(ends, b_ref[:, g * STATE : (g + 1) * STATE], 0.0).astype(bf16)
        em_ref[:, cols] = em
        state_ref[:, cols] = em[:1] * tn(b_end, xd)
        decay_ref[:, cols] = em * em * unbroken


def forward_kernel(heads, x_ref, z_ref, b_ref, c_ref, gx_ref, e_ref, einv_ref, dt_ref, rc_ref,
                   rr_ref, em_ref, skip_ref, gain_ref, down_ref, gu_ref, sin_ref,
                   mixed_ref, dz_ref, gy_ref, gd_ref, ginj_ref, pn_ref, k_ref, ddown_ref, u_ref):
    rows = x_ref.shape[0]
    groups = b_ref.shape[1] // STATE
    width = x_ref.shape[1] // groups
    per_group = heads // groups
    mask = score_mask(rc_ref[:, :1], rr_ref[:1, :])
    fresh = rc_ref[:, :1] == 0
    f_cols = dt_ref[...] * einv_ref[...]
    gu = gu_ref[...]
    u = jnp.zeros(u_ref.shape, f32)
    pn = jnp.zeros(pn_ref.shape, f32)
    kk = jnp.zeros((8, LANES), f32)
    for g in range(groups):
        cols = slice(g * width, (g + 1) * width)
        narrow = slice(g * STATE, (g + 1) * STATE)
        x = x_ref[:, cols].astype(f32)
        ex = expand(e_ref[...], g, per_group, width)
        xd = (x * expand(f_cols, g, per_group, width)).astype(bf16)
        c = c_ref[:, narrow]
        a = jnp.where(mask, nt(c, b_ref[:, narrow]), 0.0).astype(bf16)
        c0 = jnp.where(fresh, c, 0.0).astype(bf16)
        em = em_ref[:1, cols]
        s = (em * sin_ref[:, cols]).astype(bf16)
        inner = nn(a, xd) + nn(c0, s)
        y = ex * inner + skip_ref[:, cols] * x
        z = z_ref[:, cols].astype(f32)
        sig = 1.0 / (1.0 + jnp.exp(-z))
        act = z * sig
        gated = y * act
        inv = lax.rsqrt(jnp.mean(gated * gated, axis=-1, keepdims=True) + eps)
        normed = gated * inv
        gain = gain_ref[:, cols]
        mixed = (normed * gain).astype(bf16)
        mixed_ref[:, cols] = mixed
        down = down_ref[:, cols]
        u = u + nt(down, mixed)
        ddown_ref[:, cols] = nn(gu, mixed)
        gn = (gx_ref[:, cols].astype(f32) + tn(gu, down)) * gain
        gg = inv * (gn - normed * jnp.mean(gn * normed, axis=-1, keepdims=True))
        gy = gg * act
        dz_ref[:, cols] = (gg * y * sig * (1.0 + z * (1.0 - sig))).astype(bf16)
        gy_ref[:, cols] = gy
        gd = (gy * ex).astype(bf16)
        gd_ref[:, cols] = gd
        inj = tn(c0, gd)
        ginj_ref[:, cols] = em * inj
        pn = pn + headsum(gd.astype(f32) * inner, g, per_group)
        kk = kk + headsum(jnp.broadcast_to(jnp.sum(s.astype(f32) * inj, axis=0, keepdims=True), (8, width)), g, per_group)
    u_ref[...] = u
    pn_ref[...] = pn
    k_ref[...] = kk


def backward_kernel(heads, x_ref, b_ref, c_ref, e_ref, einv_ref, dt_ref, rc_ref, rr_ref, em_ref,
                    skip_ref, rate_ref, gy_ref, gd_ref, sin_ref, pn_ref, k_ref, gin_ref, decay_ref,
                    dx_ref, db_ref, dc_ref, dstep_ref):
    rows = x_ref.shape[0]
    groups = b_ref.shape[1] // STATE
    width = x_ref.shape[1] // groups
    per_group = heads // groups
    mask = score_mask(rc_ref[:, :1], rr_ref[:1, :])
    fresh = rc_ref[:, :1] == 0
    ends = rc_ref[:, :1] == rc_ref[rows - 1 : rows, :1]
    f_cols = dt_ref[...] * einv_ref[...]
    net = -pn_ref[...]
    step = jnp.zeros(pn_ref.shape, f32)
    kk = k_ref[...]
    for g in range(groups):
        cols = slice(g * width, (g + 1) * width)
        narrow = slice(g * STATE, (g + 1) * STATE)
        x = x_ref[:, cols].astype(f32)
        fx = expand(f_cols, g, per_group, width)
        xd = (x * fx).astype(bf16)
        gd = gd_ref[:, cols]
        b = b_ref[:, narrow]
        c = c_ref[:, narrow]
        a = jnp.where(mask, nt(c, b), 0.0).astype(bf16)
        b_end = jnp.where(ends, b, 0.0).astype(bf16)
        em = em_ref[:1, cols]
        sin = sin_ref[:, cols]
        gin = gin_ref[:, cols]
        s = (em * sin).astype(bf16)
        ge = (em * gin).astype(bf16)
        v = tn(a, gd) + nn(b_end, ge)
        dx_ref[:, cols] = (fx * v + skip_ref[:, cols] * gy_ref[:, cols]).astype(bf16)
        pair = jnp.where(mask, nt(gd, xd), 0.0).astype(bf16)
        dc_ref[:, narrow] = (nn(pair, b) + jnp.where(fresh, nt(gd, s), 0.0)).astype(bf16)
        db_ref[:, narrow] = (tn(pair, c) + jnp.where(ends, nt(xd, ge), 0.0)).astype(bf16)
        net = net + headsum(xd.astype(f32) * v, g, per_group)
        step = step + headsum(x * v, g, per_group)
        through = decay_ref[:1, cols] * jnp.sum(sin * gin, axis=0, keepdims=True)
        kk = kk + headsum(jnp.broadcast_to(through, (8, width)), g, per_group)
    before = jnp.where(iota((rows, rows), 0) > iota((rows, rows), 1), 1.0, 0.0)
    glog = lax.dot_general(before, net, (((1,), (0,)), ((), ())), precision=highest, preferred_element_type=f32) + kk[:1]
    gdt = einv_ref[...] * step - rate_ref[...] * glog
    out = gdt * (1.0 - jnp.exp(-dt_ref[...]))
    dstep_ref[...] = out.T[: dstep_ref.shape[0], :]


CHUNK = 16


def remote(src, dst, send, recv, target):
    return pltpu.make_async_remote_copy(
        src_ref=src, dst_ref=dst, send_sem=send, recv_sem=recv, device_id=target,
        device_id_type=pl.DeviceIdType.MESH,
    )


def group_peers():
    inner = lax.axis_size("fsdp")
    count = lax.axis_size("head") * inner
    me = lax.axis_index("head") * inner + lax.axis_index("fsdp")
    ids = [lax.rem(me + d, count) for d in range(1, count)]
    return [{"head": lax.div(i, inner), "fsdp": lax.rem(i, inner)} for i in ids]


def greet():
    ctx = lax.axis_size("ctx")
    place = lax.axis_index("ctx")
    barrier = pltpu.get_barrier_semaphore()
    peers = group_peers()
    for peer in peers:
        pl.semaphore_signal(barrier, inc=1, device_id=peer, device_id_type=pl.DeviceIdType.MESH)

    @pl.when(place > 0)
    def _():
        pl.semaphore_signal(barrier, inc=1, device_id={"ctx": place - 1}, device_id_type=pl.DeviceIdType.MESH)

    @pl.when(place < ctx - 1)
    def _():
        pl.semaphore_signal(barrier, inc=1, device_id={"ctx": place + 1}, device_id_type=pl.DeviceIdType.MESH)

    ends = (place == 0) | (place == ctx - 1)

    @pl.when(ends)
    def _():
        pl.semaphore_wait(barrier, len(peers) + 1)

    @pl.when(jnp.logical_not(ends))
    def _():
        pl.semaphore_wait(barrier, len(peers) + 2)


def exchange(part_ref, box, send, recv):
    return [remote(part_ref, box.at[d], send.at[d], recv.at[d], peer) for d, peer in enumerate(group_peers())]


def gathered_sum(part_ref, box):
    total = part_ref[...]
    for d in range(box.shape[0]):
        total = total + box[d]
    return (adapter_scale * total).astype(bf16)


def chain_step(k, first, last, target, inbox, outbox, send, recv, decay, own_ref):
    copy = remote(outbox.at[k], inbox.at[k], send.at[k], recv.at[k], target)

    @pl.when(first)
    def _():
        inbox[k] = jnp.zeros(inbox.shape[1:], f32)

    @pl.when(jnp.logical_not(first))
    def _():
        copy.wait_recv()

    @pl.when(jnp.logical_not(last))
    def _():
        outbox[k] = decay * inbox[k] + own_ref[CHUNK * k : CHUNK * (k + 1), :]
        copy.start()

    return copy


def start_kernel(part_ref, state_ref, decay_ref, gu_ref, sin_ref, box, inbox, outbox, gsend, grecv, send, recv):
    ctx = lax.axis_size("ctx")
    place = lax.axis_index("ctx")
    first, last = place == 0, place == ctx - 1
    greet()
    swaps = exchange(part_ref, box, gsend, grecv)
    decay = decay_ref[:1, :]
    target = {"ctx": lax.rem(place + 1, ctx)}
    copies = []
    for k in range(inbox.shape[0]):
        copies.append(chain_step(k, first, last, target, inbox, outbox, send, recv, decay, state_ref))
        if k == 0:
            for swap in swaps:
                swap.start()
        sin_ref[CHUNK * k : CHUNK * (k + 1), :] = inbox[k]
    for swap in swaps:
        swap.wait()
    gu_ref[...] = gathered_sum(part_ref, box)

    @pl.when(jnp.logical_not(last))
    def _():
        for copy in copies:
            copy.wait_send()


def middle_kernel(part_ref, up_ref, gout_ref, ginj_ref, decay_ref, ddown_ref,
                  gin_ref, out_ref, gdown_ref, gup_ref,
                  box, inbox, outbox, upbox, sums, downbox,
                  usend, urecv, send, recv, up_send, up_recv, dn_send, dn_recv):
    ctx = lax.axis_size("ctx")
    place = lax.axis_index("ctx")
    first, last = place == 0, place == ctx - 1
    chunks = inbox.shape[0]
    half = chunks // 2
    above = {"ctx": lax.rem(place + 1, ctx)}
    below = {"ctx": lax.rem(place + ctx - 1, ctx)}
    greet()
    swaps = exchange(part_ref, box, usend, urecv)
    ups = [remote(sums.at[k], upbox.at[k], up_send.at[k], up_recv.at[k], above) for k in range(chunks)]
    tops = [remote(sums.at[k], downbox.at[k], dn_send.at[k], dn_recv.at[k], below) for k in range(chunks)]
    downs = [remote(downbox.at[k], downbox.at[k], dn_send.at[k], dn_recv.at[k], below) for k in range(chunks)]
    for k in range(half):
        sums[k] = ddown_ref[CHUNK * k : CHUNK * (k + 1), :]

    def adapter():
        for swap in swaps:
            swap.wait()
        u = gathered_sum(part_ref, box)
        out_ref[...] = tn(u, up_ref[...]).astype(bf16)
        dup = nn(u, gout_ref[...])
        for k in range(half):
            sums[half + k] = dup[CHUNK * k : CHUNK * (k + 1), :]

    def climb(k):
        @pl.when(jnp.logical_not(first))
        def _():
            ups[k].wait_recv()
            sums[k] = sums[k] + upbox[k]

            @pl.when(jnp.logical_not(last))
            def _():
                ups[k].start()

            @pl.when(last)
            def _():
                tops[k].start()

    @pl.when(last)
    def _():
        for k in range(chunks):
            outbox[k] = ginj_ref[CHUNK * k : CHUNK * (k + 1), :]
            inbox[k] = jnp.zeros(inbox.shape[1:], f32)
            remote(outbox.at[k], inbox.at[k], send.at[k], recv.at[k], below).start()

    for swap in swaps:
        swap.start()

    @pl.when(first)
    def _():
        for k in range(half):
            ups[k].start()
        adapter()
        for k in range(half, chunks):
            ups[k].start()

    decay = decay_ref[:1, :]
    copies = [remote(outbox.at[k], inbox.at[k], send.at[k], recv.at[k], below) for k in range(chunks)]
    for k in range(chunks):

        @pl.when(jnp.logical_not(last))
        def _():
            copies[k].wait_recv()

            @pl.when(jnp.logical_not(first))
            def _():
                outbox[k] = decay * inbox[k] + ginj_ref[CHUNK * k : CHUNK * (k + 1), :]
                copies[k].start()

        if k >= half:
            climb(k - half)
        gin_ref[CHUNK * k : CHUNK * (k + 1), :] = inbox[k]

    @pl.when(jnp.logical_not(first))
    def _():
        adapter()

    for k in range(half, chunks):
        climb(k)

    for k in range(chunks):

        @pl.when(jnp.logical_not(last))
        def _():
            downs[k].wait_recv()
            sums_k = downbox[k]

            @pl.when(jnp.logical_not(first))
            def _():
                downs[k].start()
                ups[k].wait_send()

            @pl.when(first)
            def _():
                ups[k].wait_send()

            sums[k] = sums_k

    gup_ref[...] = jnp.concatenate([sums[half + k] for k in range(half)], axis=0)
    gdown_ref[...] = jnp.concatenate([sums[k] for k in range(half)], axis=0).T

    @pl.when(jnp.logical_not(first))
    def _():
        for k in range(chunks):
            copies[k].wait_send()
            downs[k].wait_send()


def call(kernel, name, outs, args, scratch=(), collective_id=None):
    params = {} if collective_id is None else dict(collective_id=collective_id, has_side_effects=True)
    whole = pl.BlockSpec(memory_space=pltpu.VMEM)
    return pl.pallas_call(
        kernel,
        name=name,
        out_shape=[jax.ShapeDtypeStruct(s, d) for s, d in outs],
        in_specs=[whole] * len(args),
        out_specs=[whole] * len(outs),
        scratch_shapes=list(scratch),
        compiler_params=pltpu.CompilerParams(vmem_limit_bytes=56 << 20, **params),
    )(*args)


def per_device(x, z, b, c, dtin, resets, rate, bias, skip, gain, down, up, gx, gout):
    rows, channels = x.shape
    heads = dtin.shape[0]
    rank = down.shape[1]
    head_dim = channels // heads
    peers = lax.axis_size("head") * lax.axis_size("fsdp") - 1
    chunks = STATE // CHUNK
    assert 2 * rank == STATE
    dma = pltpu.SemaphoreType.DMA
    slab = pltpu.VMEM((chunks, CHUNK, channels), f32)
    swap = pltpu.VMEM((peers, rank, rows), f32)
    skip_row = jnp.repeat(skip, head_dim)[None, :]
    gain_row = gain[None, :]
    rate_row = jnp.pad(rate, (0, LANES - heads))[None, :]
    down_rows = down.T
    e, einv, dt, rc, rr, em, decay, state = call(
        scan_kernel, "scan",
        [((rows, LANES), f32)] * 4 + [((8, rows), f32), ((8, channels), f32), ((8, channels), f32), ((STATE, channels), f32)],
        (x, b, dtin, bias[:, None], rate[:, None], resets[None, :]),
    )
    gu_part = nt(up, gout)
    gu, sin = call(
        start_kernel, "start", [((rank, rows), bf16), ((STATE, channels), f32)], (gu_part, state, decay),
        [swap, slab, slab, dma((peers,)), dma((peers,)), dma((chunks,)), dma((chunks,))], 1,
    )
    mixed, dz, gy, gd, ginj, pn, kk, ddown, u_part = call(
        lambda *r: forward_kernel(heads, *r), "forward",
        [((rows, channels), bf16), ((rows, channels), bf16), ((rows, channels), f32), ((rows, channels), bf16),
         ((STATE, channels), f32), ((rows, LANES), f32), ((8, LANES), f32),
         ((rank, channels), f32), ((rank, rows), f32)],
        (x, z, b, c, gx, e, einv, dt, rc, rr, em, skip_row, gain_row, down_rows, gu, sin),
    )
    gin, adapter_output, gdown, gup = call(
        middle_kernel, "middle",
        [((STATE, channels), f32), ((rows, channels), bf16), ((channels, rank), f32), ((rank, channels), f32)],
        (u_part, up, gout, ginj, decay, ddown),
        [swap] + [slab] * 5 + [dma((peers,))] * 2 + [dma((chunks,))] * 6, 2,
    )
    dx, db, dc, dstep = call(
        lambda *r: backward_kernel(heads, *r), "backward",
        [((rows, channels), bf16), (b.shape, bf16), (c.shape, bf16), ((heads, rows), f32)],
        (x, b, c, e, einv, dt, rc, rr, em, skip_row, rate_row, gy, gd, sin, pn, kk, gin, decay),
    )
    return mixed, adapter_output, dx, dz, db, dc, dstep, gdown, gup


def solution(mesh):
    wide = P(("parts", "ctx"), ("head", "fsdp"))
    steps = P(("head", "fsdp"), ("parts", "ctx"))
    over_heads = P(("head", "fsdp"))
    in_specs = (
        wide, wide, wide, wide, steps, P(("parts", "ctx")), over_heads, over_heads, over_heads, over_heads,
        P(("head", "fsdp"), None), P(None, ("head", "fsdp")), wide, wide,
    )
    out_specs = (
        wide, wide, wide, wide, wide, wide, steps, P(("parts", "head", "fsdp"), None), P("parts", ("head", "fsdp")),
    )
    return jax.shard_map(per_device, mesh=mesh, in_specs=in_specs, out_specs=out_specs, check_vma=False)
```

```python
import jax
import jax.numpy as jnp
from jax import lax
from jax.experimental import pallas as pl
from jax.experimental.pallas import tpu as pltpu
from jax.sharding import PartitionSpec as P

STATE = 128
LANES = 128
eps = 1e-05
adapter_scale = 2.0
highest = lax.Precision.HIGHEST
f32 = jnp.float32
bf16 = jnp.bfloat16


def nn(a, b):
    return lax.dot_general(a, b, (((1,), (0,)), ((), ())), preferred_element_type=f32)


def nt(a, b):
    return lax.dot_general(a, b, (((1,), (1,)), ((), ())), preferred_element_type=f32)


def tn(a, b):
    return lax.dot_general(a, b, (((0,), (0,)), ((), ())), preferred_element_type=f32)


def split(a):
    hi = a.astype(bf16)
    return hi, (a - hi.astype(f32)).astype(bf16)


def iota(shape, dim):
    return lax.broadcasted_iota(jnp.int32, shape, dim)


def expand(cols, group, per_group, width):
    pick = (iota((LANES, width), 0) == group * per_group + iota((LANES, width), 1) // (width // per_group))
    pick = jnp.where(pick, 1.0, 0.0).astype(bf16)
    hi, lo = split(cols)
    return nn(hi, pick) + nn(lo, pick)


def headsum(values, group, per_group):
    width = values.shape[1]
    pick = (iota((width, LANES), 1) == group * per_group + iota((width, LANES), 0) // (width // per_group))
    pick = jnp.where(pick, 1.0, 0.0).astype(bf16)
    hi, lo = split(values)
    return nn(hi, pick) + nn(lo, pick)


def padded(row):
    return jnp.concatenate([row, jnp.zeros((1, LANES - row.shape[1]), f32)], axis=1)


def tall(row):
    return jnp.broadcast_to(padded(row), (LANES, LANES)).T[: row.shape[1], :1]


def wide_row(row, group, per_group, width):
    return expand(jnp.broadcast_to(padded(row), (8, LANES)), group, per_group, width)[:1]


def score_mask(rid_col, rid_row):
    n = rid_col.shape[0]
    return (rid_col == rid_row) & (iota((n, n), 0) >= iota((n, n), 1))


def scan_kernel(x_ref, b_ref, dtin_ref, bias_ref, rate_ref, resets_ref,
                e_ref, einv_ref, dt_ref, rc_ref, rr_ref, em_ref, decay_ref, state_ref):
    rows = x_ref.shape[0]
    heads = dtin_ref.shape[0]
    groups = b_ref.shape[1] // STATE
    per_group = heads // groups
    width = x_ref.shape[1] // groups
    v = dtin_ref[...] + tall(bias_ref[...])
    dt = jnp.maximum(v, 0.0) + jnp.log1p(jnp.exp(-jnp.abs(v)))
    log_step = -tall(rate_ref[...]) * dt
    marks = jnp.broadcast_to(resets_ref[...].astype(f32), (8, rows))
    stack = jnp.concatenate([log_step, marks, jnp.zeros((LANES - heads - 8, rows), f32)], axis=0)
    dt_cols = jnp.concatenate([dt, jnp.zeros((LANES - heads, rows), f32)], axis=0).T
    tri = jnp.where(iota((rows, rows), 0) >= iota((rows, rows), 1), 1.0, 0.0)
    cum = lax.dot_general(tri, stack.T, (((1,), (0,)), ((), ())), precision=highest, preferred_element_type=f32)
    cum_rows = cum.T
    rid_col = cum[:, heads : heads + 1]
    rid_row = cum_rows[heads : heads + 1, :]
    rid_last = cum[rows - 1 : rows, heads : heads + 1]
    cum_heads = jnp.where(iota((rows, LANES), 1) < heads, cum, 0.0)
    mid = 0.5 * cum_heads[rows - 1 : rows, :]
    e_ref[...] = jnp.exp(cum_heads - mid)
    einv = jnp.exp(mid - cum_heads)
    einv_ref[...] = einv
    dt_ref[...] = dt_cols
    f_cols = dt_cols * einv
    rc_ref[...] = jnp.broadcast_to(rid_col, rc_ref.shape)
    rr_ref[...] = jnp.broadcast_to(rid_row, rr_ref.shape)
    ends = rid_col == rid_last
    unbroken = jnp.where(rid_last == 0, 1.0, 0.0)
    em_cols = jnp.broadcast_to(jnp.exp(mid), (8, LANES))
    for g in range(groups):
        cols = slice(g * width, (g + 1) * width)
        em = expand(em_cols, g, per_group, width)
        xd = (x_ref[:, cols].astype(f32) * expand(f_cols, g, per_group, width)).astype(bf16)
        b_end = jnp.where(ends, b_ref[:, g * STATE : (g + 1) * STATE], 0.0).astype(bf16)
        em_ref[:, cols] = em
        state_ref[:, cols] = em[:1] * tn(b_end, xd)
        decay_ref[:, cols] = em * em * unbroken


def forward_kernel(heads, x_ref, z_ref, b_ref, c_ref, gx_ref, e_ref, einv_ref, dt_ref, rc_ref,
                   rr_ref, em_ref, skip_ref, gain_ref, down_ref, gu_ref, sin_ref,
                   mixed_ref, dz_ref, gy_ref, gd_ref, ginj_ref, pn_ref, k_ref, ddown_ref, u_ref):
    rows = x_ref.shape[0]
    groups = b_ref.shape[1] // STATE
    width = x_ref.shape[1] // groups
    per_group = heads // groups
    mask = score_mask(rc_ref[:, :1], rr_ref[:1, :])
    fresh = rc_ref[:, :1] == 0
    f_cols = dt_ref[...] * einv_ref[...]
    gu = gu_ref[...]
    u = jnp.zeros(u_ref.shape, f32)
    pn = jnp.zeros(pn_ref.shape, f32)
    kk = jnp.zeros((8, LANES), f32)
    for g in range(groups):
        cols = slice(g * width, (g + 1) * width)
        narrow = slice(g * STATE, (g + 1) * STATE)
        x = x_ref[:, cols].astype(f32)
        ex = expand(e_ref[...], g, per_group, width)
        xd = (x * expand(f_cols, g, per_group, width)).astype(bf16)
        c = c_ref[:, narrow]
        a = jnp.where(mask, nt(c, b_ref[:, narrow]), 0.0).astype(bf16)
        c0 = jnp.where(fresh, c, 0.0).astype(bf16)
        em = em_ref[:1, cols]
        s = (em * sin_ref[:, cols]).astype(bf16)
        inner = nn(a, xd) + nn(c0, s)
        y = ex * inner + wide_row(skip_ref[...], g, per_group, width) * x
        z = z_ref[:, cols].astype(f32)
        sig = 1.0 / (1.0 + jnp.exp(-z))
        act = z * sig
        gated = y * act
        inv = lax.rsqrt(jnp.mean(gated * gated, axis=-1, keepdims=True) + eps)
        normed = gated * inv
        gain = gain_ref[:, cols]
        mixed = (normed * gain).astype(bf16)
        mixed_ref[:, cols] = mixed
        down = down_ref[:, cols]
        u = u + nt(down, mixed)
        ddown_ref[:, cols] = nn(gu, mixed)
        gn = (gx_ref[:, cols].astype(f32) + tn(gu, down)) * gain
        gg = inv * (gn - normed * jnp.mean(gn * normed, axis=-1, keepdims=True))
        gy = gg * act
        dz_ref[:, cols] = (gg * y * sig * (1.0 + z * (1.0 - sig))).astype(bf16)
        gy_ref[:, cols] = gy
        gd = (gy * ex).astype(bf16)
        gd_ref[:, cols] = gd
        inj = tn(c0, gd)
        ginj_ref[:, cols] = em * inj
        pn = pn + headsum(gd.astype(f32) * inner, g, per_group)
        kk = kk + headsum(jnp.broadcast_to(jnp.sum(s.astype(f32) * inj, axis=0, keepdims=True), (8, width)), g, per_group)
    u_ref[...] = u
    pn_ref[...] = pn
    k_ref[...] = kk


def backward_kernel(heads, x_ref, b_ref, c_ref, e_ref, einv_ref, dt_ref, rc_ref, rr_ref, em_ref,
                    skip_ref, rate_ref, gy_ref, gd_ref, sin_ref, pn_ref, k_ref, gin_ref, decay_ref, ddown_ref, dup_ref,
                    dx_ref, db_ref, dc_ref, dstep_ref, gdown_ref, gup_ref,
                    mine, arrived, totals, send, recv, back_send, back_recv):
    rows = x_ref.shape[0]
    groups = b_ref.shape[1] // STATE
    width = x_ref.shape[1] // groups
    per_group = heads // groups
    ctx = lax.axis_size("ctx")
    place = lax.axis_index("ctx")
    share = mine.shape[1]
    rank = ddown_ref.shape[0]
    others = [lax.rem(place + d, ctx) for d in range(1, ctx)]
    barrier = pltpu.get_barrier_semaphore()
    for other in others:
        pl.semaphore_signal(barrier, inc=1, device_id={"ctx": other}, device_id_type=pl.DeviceIdType.MESH)
    for j in range(ctx):
        lo = j * share
        mine[j] = ddown_ref[lo : lo + share, :] if lo < rank else dup_ref[lo - rank : lo - rank + share, :]
    pl.semaphore_wait(barrier, ctx - 1)
    out_copies = [
        remote(mine.at[j], arrived.at[d], send.at[d], recv.at[d], {"ctx": j}) for d, j in enumerate(others)
    ]
    back_copies = [
        remote(totals.at[place], totals.at[place], back_send.at[d], back_recv.at[d], {"ctx": j})
        for d, j in enumerate(others)
    ]
    for copy in out_copies:
        copy.start()
    mask = score_mask(rc_ref[:, :1], rr_ref[:1, :])
    fresh = rc_ref[:, :1] == 0
    ends = rc_ref[:, :1] == rc_ref[rows - 1 : rows, :1]
    f_cols = dt_ref[...] * einv_ref[...]
    net = -pn_ref[...]
    step = jnp.zeros(pn_ref.shape, f32)
    kk = k_ref[...]
    for g in range(groups):
        cols = slice(g * width, (g + 1) * width)
        narrow = slice(g * STATE, (g + 1) * STATE)
        x = x_ref[:, cols].astype(f32)
        fx = expand(f_cols, g, per_group, width)
        xd = (x * fx).astype(bf16)
        gd = gd_ref[:, cols]
        b = b_ref[:, narrow]
        c = c_ref[:, narrow]
        a = jnp.where(mask, nt(c, b), 0.0).astype(bf16)
        b_end = jnp.where(ends, b, 0.0).astype(bf16)
        em = em_ref[:1, cols]
        sin = sin_ref[:, cols]
        gin = gin_ref[:, cols]
        s = (em * sin).astype(bf16)
        ge = (em * gin).astype(bf16)
        v = tn(a, gd) + nn(b_end, ge)
        dx_ref[:, cols] = (fx * v + wide_row(skip_ref[...], g, per_group, width) * gy_ref[:, cols]).astype(bf16)
        pair = jnp.where(mask, nt(gd, xd), 0.0).astype(bf16)
        dc_ref[:, narrow] = (nn(pair, b) + jnp.where(fresh, nt(gd, s), 0.0)).astype(bf16)
        db_ref[:, narrow] = (tn(pair, c) + jnp.where(ends, nt(xd, ge), 0.0)).astype(bf16)
        net = net + headsum(xd.astype(f32) * v, g, per_group)
        step = step + headsum(x * v, g, per_group)
        through = decay_ref[:1, cols] * jnp.sum(sin * gin, axis=0, keepdims=True)
        kk = kk + headsum(jnp.broadcast_to(through, (8, width)), g, per_group)
        if g == 0:
            total = mine[place]
            for d, copy in enumerate(out_copies):
                copy.wait()
                total = total + arrived[d]
            totals[place] = total
            for copy in back_copies:
                copy.start()
    before = jnp.where(iota((rows, rows), 0) > iota((rows, rows), 1), 1.0, 0.0)
    glog = lax.dot_general(before, net, (((1,), (0,)), ((), ())), precision=highest, preferred_element_type=f32) + kk[:1]
    gdt = einv_ref[...] * step - padded(rate_ref[...]) * glog
    out = gdt * (1.0 - jnp.exp(-dt_ref[...]))
    dstep_ref[...] = out.T[: dstep_ref.shape[0], :]
    for copy in back_copies:
        copy.wait()
    gdown_ref[...] = jnp.concatenate([totals[j] for j in range(ctx // 2)], axis=0).T
    gup_ref[...] = jnp.concatenate([totals[j] for j in range(ctx // 2, ctx)], axis=0)


CHUNK = 16


def remote(src, dst, send, recv, target):
    return pltpu.make_async_remote_copy(
        src_ref=src, dst_ref=dst, send_sem=send, recv_sem=recv, device_id=target,
        device_id_type=pl.DeviceIdType.MESH,
    )


def group_peers():
    inner = lax.axis_size("fsdp")
    count = lax.axis_size("head") * inner
    me = lax.axis_index("head") * inner + lax.axis_index("fsdp")
    ids = [lax.rem(me + d, count) for d in range(1, count)]
    return [{"head": lax.div(i, inner), "fsdp": lax.rem(i, inner)} for i in ids]


def greet():
    ctx = lax.axis_size("ctx")
    place = lax.axis_index("ctx")
    barrier = pltpu.get_barrier_semaphore()
    peers = group_peers()
    for peer in peers:
        pl.semaphore_signal(barrier, inc=1, device_id=peer, device_id_type=pl.DeviceIdType.MESH)

    @pl.when(place > 0)
    def _():
        pl.semaphore_signal(barrier, inc=1, device_id={"ctx": place - 1}, device_id_type=pl.DeviceIdType.MESH)

    @pl.when(place < ctx - 1)
    def _():
        pl.semaphore_signal(barrier, inc=1, device_id={"ctx": place + 1}, device_id_type=pl.DeviceIdType.MESH)

    ends = (place == 0) | (place == ctx - 1)

    @pl.when(ends)
    def _():
        pl.semaphore_wait(barrier, len(peers) + 1)

    @pl.when(jnp.logical_not(ends))
    def _():
        pl.semaphore_wait(barrier, len(peers) + 2)


def exchange(part_ref, box, send, recv):
    return [remote(part_ref, box.at[d], send.at[d], recv.at[d], peer) for d, peer in enumerate(group_peers())]


def gathered_sum(part_ref, box):
    total = part_ref[...]
    for d in range(box.shape[0]):
        total = total + box[d]
    return (adapter_scale * total).astype(bf16)


def chain_step(k, first, last, target, inbox, outbox, send, recv, decay, own_ref):
    copy = remote(outbox.at[k], inbox.at[k], send.at[k], recv.at[k], target)

    @pl.when(first)
    def _():
        inbox[k] = jnp.zeros(inbox.shape[1:], f32)

    @pl.when(jnp.logical_not(first))
    def _():
        copy.wait_recv()

    @pl.when(jnp.logical_not(last))
    def _():
        outbox[k] = decay * inbox[k] + own_ref[CHUNK * k : CHUNK * (k + 1), :]
        copy.start()

    return copy


def start_kernel(part_ref, state_ref, decay_ref, gu_ref, sin_ref, box, inbox, outbox, gsend, grecv, send, recv):
    ctx = lax.axis_size("ctx")
    place = lax.axis_index("ctx")
    first, last = place == 0, place == ctx - 1
    greet()
    swaps = exchange(part_ref, box, gsend, grecv)
    decay = decay_ref[:1, :]
    target = {"ctx": lax.rem(place + 1, ctx)}
    copies = []
    for k in range(inbox.shape[0]):
        copies.append(chain_step(k, first, last, target, inbox, outbox, send, recv, decay, state_ref))
        if k == 0:
            for swap in swaps:
                swap.start()
        sin_ref[CHUNK * k : CHUNK * (k + 1), :] = inbox[k]
    for swap in swaps:
        swap.wait()
    gu_ref[...] = gathered_sum(part_ref, box)

    @pl.when(jnp.logical_not(last))
    def _():
        for copy in copies:
            copy.wait_send()


def middle_kernel(part_ref, up_ref, gout_ref, ginj_ref, decay_ref, gin_ref, out_ref, dup_ref,
                  box, inbox, outbox, usend, urecv, send, recv):
    ctx = lax.axis_size("ctx")
    place = lax.axis_index("ctx")
    first, last = place == 0, place == ctx - 1
    chunks = inbox.shape[0]
    below = {"ctx": lax.rem(place + ctx - 1, ctx)}
    greet()
    swaps = exchange(part_ref, box, usend, urecv)
    copies = [remote(outbox.at[k], inbox.at[k], send.at[k], recv.at[k], below) for k in range(chunks)]

    def adapter():
        for swap in swaps:
            swap.wait()
        u = gathered_sum(part_ref, box)
        out_ref[...] = tn(u, up_ref[...]).astype(bf16)
        dup_ref[...] = nn(u, gout_ref[...])

    @pl.when(last)
    def _():
        for k in range(chunks):
            outbox[k] = ginj_ref[CHUNK * k : CHUNK * (k + 1), :]
            copies[k].start()
        gin_ref[...] = jnp.zeros_like(gin_ref)

    for swap in swaps:
        swap.start()

    @pl.when(first)
    def _():
        adapter()

    decay = decay_ref[:1, :]

    @pl.when(jnp.logical_not(last))
    def _():
        for k in range(chunks):
            copies[k].wait_recv()

            @pl.when(jnp.logical_not(first))
            def _():
                outbox[k] = decay * inbox[k] + ginj_ref[CHUNK * k : CHUNK * (k + 1), :]
                copies[k].start()

            gin_ref[CHUNK * k : CHUNK * (k + 1), :] = inbox[k]

    @pl.when(jnp.logical_not(first))
    def _():
        adapter()
        for k in range(chunks):
            copies[k].wait_send()


def call(kernel, name, outs, args, scratch=(), collective_id=None):
    params = {} if collective_id is None else dict(collective_id=collective_id, has_side_effects=True)
    whole = pl.BlockSpec(memory_space=pltpu.VMEM)
    return pl.pallas_call(
        kernel,
        name=name,
        out_shape=[jax.ShapeDtypeStruct(s, d) for s, d in outs],
        in_specs=[whole] * len(args),
        out_specs=[whole] * len(outs),
        scratch_shapes=list(scratch),
        compiler_params=pltpu.CompilerParams(vmem_limit_bytes=56 << 20, **params),
    )(*args)


def per_device(x, z, b, c, dtin, resets, rate, bias, skip, gain, down, up, gx, gout):
    rows, channels = x.shape
    heads = dtin.shape[0]
    rank = down.shape[1]
    peers = lax.axis_size("head") * lax.axis_size("fsdp") - 1
    chunks = STATE // CHUNK
    assert 2 * rank == STATE
    dma = pltpu.SemaphoreType.DMA
    slab = pltpu.VMEM((chunks, CHUNK, channels), f32)
    swap = pltpu.VMEM((peers, rank, rows), f32)
    skip_row = skip[None, :]
    gain_row = gain[None, :]
    rate_row = rate[None, :]
    down_rows = down.T
    e, einv, dt, rc, rr, em, decay, state = call(
        scan_kernel, "scan",
        [((rows, LANES), f32)] * 4 + [((8, rows), f32), ((8, channels), f32), ((8, channels), f32), ((STATE, channels), f32)],
        (x, b, dtin, bias[None, :], rate_row, resets[None, :]),
    )
    gu_part = nt(up, gout)
    gu, sin = call(
        start_kernel, "start", [((rank, rows), bf16), ((STATE, channels), f32)], (gu_part, state, decay),
        [swap, slab, slab, dma((peers,)), dma((peers,)), dma((chunks,)), dma((chunks,))], 1,
    )
    mixed, dz, gy, gd, ginj, pn, kk, ddown, u_part = call(
        lambda *r: forward_kernel(heads, *r), "forward",
        [((rows, channels), bf16), ((rows, channels), bf16), ((rows, channels), f32), ((rows, channels), bf16),
         ((STATE, channels), f32), ((rows, LANES), f32), ((8, LANES), f32),
         ((rank, channels), f32), ((rank, rows), f32)],
        (x, z, b, c, gx, e, einv, dt, rc, rr, em, skip_row, gain_row, down_rows, gu, sin),
    )
    gin, adapter_output, dup = call(
        middle_kernel, "middle",
        [((STATE, channels), f32), ((rows, channels), bf16), ((rank, channels), f32)],
        (u_part, up, gout, ginj, decay),
        [swap, slab, slab] + [dma((peers,))] * 2 + [dma((chunks,))] * 2, 2,
    )
    ctx = lax.axis_size("ctx")
    share = STATE // ctx
    dx, db, dc, dstep, gdown, gup = call(
        lambda *r: backward_kernel(heads, *r), "backward",
        [((rows, channels), bf16), (b.shape, bf16), (c.shape, bf16), ((heads, rows), f32),
         ((channels, rank), f32), ((rank, channels), f32)],
        (x, b, c, e, einv, dt, rc, rr, em, skip_row, rate_row, gy, gd, sin, pn, kk, gin, decay, ddown, dup),
        [pltpu.VMEM((ctx, share, channels), f32), pltpu.VMEM((ctx - 1, share, channels), f32),
         pltpu.VMEM((ctx, share, channels), f32)] + [dma((ctx - 1,))] * 4, 3,
    )
    return mixed, adapter_output, dx, dz, db, dc, dstep, gdown, gup


def solution(mesh):
    wide = P(("parts", "ctx"), ("head", "fsdp"))
    steps = P(("head", "fsdp"), ("parts", "ctx"))
    over_heads = P(("head", "fsdp"))
    in_specs = (
        wide, wide, wide, wide, steps, P(("parts", "ctx")), over_heads, over_heads, over_heads, over_heads,
        P(("head", "fsdp"), None), P(None, ("head", "fsdp")), wide, wide,
    )
    out_specs = (
        wide, wide, wide, wide, wide, wide, steps, P(("parts", "head", "fsdp"), None), P("parts", ("head", "fsdp")),
    )
    return jax.shard_map(per_device, mesh=mesh, in_specs=in_specs, out_specs=out_specs, check_vma=False)
```

```python
import jax
import jax.numpy as jnp
from jax import lax
from jax.experimental import pallas as pl
from jax.experimental.pallas import tpu as pltpu
from jax.sharding import PartitionSpec as P

STATE = 128
LANES = 128
eps = 1e-05
adapter_scale = 2.0
highest = lax.Precision.HIGHEST
f32 = jnp.float32
bf16 = jnp.bfloat16


def nn(a, b):
    return lax.dot_general(a, b, (((1,), (0,)), ((), ())), preferred_element_type=f32)


def nt(a, b):
    return lax.dot_general(a, b, (((1,), (1,)), ((), ())), preferred_element_type=f32)


def tn(a, b):
    return lax.dot_general(a, b, (((0,), (0,)), ((), ())), preferred_element_type=f32)


def split(a):
    hi = a.astype(bf16)
    return hi, (a - hi.astype(f32)).astype(bf16)


def iota(shape, dim):
    return lax.broadcasted_iota(jnp.int32, shape, dim)


def expand(cols, group, per_group, width):
    pick = (iota((LANES, width), 0) == group * per_group + iota((LANES, width), 1) // (width // per_group))
    pick = jnp.where(pick, 1.0, 0.0).astype(bf16)
    hi, lo = split(cols)
    return nn(hi, pick) + nn(lo, pick)


def headsum(values, group, per_group):
    width = values.shape[1]
    pick = (iota((width, LANES), 1) == group * per_group + iota((width, LANES), 0) // (width // per_group))
    pick = jnp.where(pick, 1.0, 0.0).astype(bf16)
    hi, lo = split(values)
    return nn(hi, pick) + nn(lo, pick)


def padded(row):
    return jnp.concatenate([row, jnp.zeros((1, LANES - row.shape[1]), f32)], axis=1)


def tall(row):
    return jnp.broadcast_to(padded(row), (LANES, LANES)).T[: row.shape[1], :1]


def wide_row(row, group, per_group, width):
    return expand(jnp.broadcast_to(padded(row), (8, LANES)), group, per_group, width)[:1]


def score_mask(rid_col, rid_row):
    n = rid_col.shape[0]
    return (rid_col == rid_row) & (iota((n, n), 0) >= iota((n, n), 1))


def scan_kernel(x_ref, b_ref, dtin_ref, bias_ref, rate_ref, resets_ref,
                e_ref, einv_ref, dt_ref, rc_ref, rr_ref, em_ref, decay_ref, state_ref):
    rows = x_ref.shape[0]
    heads = dtin_ref.shape[0]
    groups = b_ref.shape[1] // STATE
    per_group = heads // groups
    width = x_ref.shape[1] // groups
    v = dtin_ref[...] + tall(bias_ref[...])
    dt = jnp.maximum(v, 0.0) + jnp.log1p(jnp.exp(-jnp.abs(v)))
    log_step = -tall(rate_ref[...]) * dt
    marks = jnp.broadcast_to(resets_ref[...].astype(f32), (8, rows))
    stack = jnp.concatenate([log_step, marks, jnp.zeros((LANES - heads - 8, rows), f32)], axis=0)
    dt_cols = jnp.concatenate([dt, jnp.zeros((LANES - heads, rows), f32)], axis=0).T
    tri = jnp.where(iota((rows, rows), 0) >= iota((rows, rows), 1), 1.0, 0.0)
    cum = lax.dot_general(tri, stack.T, (((1,), (0,)), ((), ())), precision=highest, preferred_element_type=f32)
    cum_rows = cum.T
    rid_col = cum[:, heads : heads + 1]
    rid_row = cum_rows[heads : heads + 1, :]
    rid_last = cum[rows - 1 : rows, heads : heads + 1]
    cum_heads = jnp.where(iota((rows, LANES), 1) < heads, cum, 0.0)
    mid = 0.5 * cum_heads[rows - 1 : rows, :]
    e_ref[...] = jnp.exp(cum_heads - mid)
    einv = jnp.exp(mid - cum_heads)
    einv_ref[...] = einv
    dt_ref[...] = dt_cols
    f_cols = dt_cols * einv
    rc_ref[...] = jnp.broadcast_to(rid_col, rc_ref.shape)
    rr_ref[...] = jnp.broadcast_to(rid_row, rr_ref.shape)
    ends = rid_col == rid_last
    unbroken = jnp.where(rid_last == 0, 1.0, 0.0)
    em_cols = jnp.broadcast_to(jnp.exp(mid), (8, LANES))
    for g in range(groups):
        cols = slice(g * width, (g + 1) * width)
        em = expand(em_cols, g, per_group, width)
        xd = (x_ref[:, cols].astype(f32) * expand(f_cols, g, per_group, width)).astype(bf16)
        b_end = jnp.where(ends, b_ref[:, g * STATE : (g + 1) * STATE], 0.0).astype(bf16)
        em_ref[:, cols] = em
        state_ref[:, cols] = em[:1] * tn(b_end, xd)
        decay_ref[:, cols] = em * em * unbroken


def forward_kernel(heads, x_ref, z_ref, b_ref, c_ref, gx_ref, e_ref, einv_ref, dt_ref, rc_ref,
                   rr_ref, em_ref, skip_ref, gain_ref, down_ref, gu_ref, sin_ref,
                   mixed_ref, dz_ref, gy_ref, gd_ref, ginj_ref, pn_ref, k_ref, ddown_ref, u_ref):
    rows = x_ref.shape[0]
    groups = b_ref.shape[1] // STATE
    width = x_ref.shape[1] // groups
    per_group = heads // groups
    mask = score_mask(rc_ref[:, :1], rr_ref[:1, :])
    fresh = rc_ref[:, :1] == 0
    f_cols = dt_ref[...] * einv_ref[...]
    gu = gu_ref[...]
    u = jnp.zeros(u_ref.shape, f32)
    pn = jnp.zeros(pn_ref.shape, f32)
    kk = jnp.zeros((8, LANES), f32)
    for g in range(groups):
        cols = slice(g * width, (g + 1) * width)
        narrow = slice(g * STATE, (g + 1) * STATE)
        x = x_ref[:, cols].astype(f32)
        ex = expand(e_ref[...], g, per_group, width)
        xd = (x * expand(f_cols, g, per_group, width)).astype(bf16)
        c = c_ref[:, narrow]
        a = jnp.where(mask, nt(c, b_ref[:, narrow]), 0.0).astype(bf16)
        c0 = jnp.where(fresh, c, 0.0).astype(bf16)
        em = em_ref[:1, cols]
        s = (em * sin_ref[:, cols]).astype(bf16)
        inner = nn(a, xd) + nn(c0, s)
        y = ex * inner + wide_row(skip_ref[...], g, per_group, width) * x
        z = z_ref[:, cols].astype(f32)
        sig = 1.0 / (1.0 + jnp.exp(-z))
        act = z * sig
        gated = y * act
        inv = lax.rsqrt(jnp.mean(gated * gated, axis=-1, keepdims=True) + eps)
        normed = gated * inv
        gain = gain_ref[:, cols]
        mixed = (normed * gain).astype(bf16)
        mixed_ref[:, cols] = mixed
        down = down_ref[:, cols]
        u = u + nt(down, mixed)
        ddown_ref[:, cols] = nn(gu, mixed)
        gn = (gx_ref[:, cols].astype(f32) + tn(gu, down)) * gain
        gg = inv * (gn - normed * jnp.mean(gn * normed, axis=-1, keepdims=True))
        gy = gg * act
        dz_ref[:, cols] = (gg * y * sig * (1.0 + z * (1.0 - sig))).astype(bf16)
        gy_ref[:, cols] = gy
        gd = (gy * ex).astype(bf16)
        gd_ref[:, cols] = gd
        inj = tn(c0, gd)
        ginj_ref[:, cols] = em * inj
        pn = pn + headsum(gd.astype(f32) * inner, g, per_group)
        kk = kk + headsum(jnp.broadcast_to(jnp.sum(s.astype(f32) * inj, axis=0, keepdims=True), (8, width)), g, per_group)
    u_ref[...] = u
    pn_ref[...] = pn
    k_ref[...] = kk


CHUNK = 8


def remote(src, dst, send, recv, target):
    return pltpu.make_async_remote_copy(
        src_ref=src, dst_ref=dst, send_sem=send, recv_sem=recv, device_id=target,
        device_id_type=pl.DeviceIdType.MESH,
    )


def group_peers():
    inner = lax.axis_size("fsdp")
    count = lax.axis_size("head") * inner
    me = lax.axis_index("head") * inner + lax.axis_index("fsdp")
    ids = [lax.rem(me + d, count) for d in range(1, count)]
    return [{"head": lax.div(i, inner), "fsdp": lax.rem(i, inner)} for i in ids]


def greet():
    ctx = lax.axis_size("ctx")
    place = lax.axis_index("ctx")
    barrier = pltpu.get_barrier_semaphore()
    peers = group_peers()
    for peer in peers:
        pl.semaphore_signal(barrier, inc=1, device_id=peer, device_id_type=pl.DeviceIdType.MESH)

    @pl.when(place > 0)
    def _():
        pl.semaphore_signal(barrier, inc=1, device_id={"ctx": place - 1}, device_id_type=pl.DeviceIdType.MESH)

    @pl.when(place < ctx - 1)
    def _():
        pl.semaphore_signal(barrier, inc=1, device_id={"ctx": place + 1}, device_id_type=pl.DeviceIdType.MESH)

    ends = (place == 0) | (place == ctx - 1)

    @pl.when(ends)
    def _():
        pl.semaphore_wait(barrier, len(peers) + 1)

    @pl.when(jnp.logical_not(ends))
    def _():
        pl.semaphore_wait(barrier, len(peers) + 2)


def exchange(part_ref, box, send, recv):
    return [remote(part_ref, box.at[d], send.at[d], recv.at[d], peer) for d, peer in enumerate(group_peers())]


def gathered_sum(part_ref, box):
    total = part_ref[...]
    for d in range(box.shape[0]):
        total = total + box[d]
    return (adapter_scale * total).astype(bf16)


def chain_step(k, first, last, target, inbox, outbox, send, recv, decay, own_ref):
    copy = remote(outbox.at[k], inbox.at[k], send.at[k], recv.at[k], target)

    @pl.when(first)
    def _():
        inbox[k] = jnp.zeros(inbox.shape[1:], f32)

    @pl.when(jnp.logical_not(first))
    def _():
        copy.wait_recv()

    @pl.when(jnp.logical_not(last))
    def _():
        outbox[k] = decay * inbox[k] + own_ref[CHUNK * k : CHUNK * (k + 1), :]
        copy.start()

    return copy


def start_kernel(part_ref, state_ref, decay_ref, gu_ref, sin_ref, box, inbox, outbox, gsend, grecv, send, recv):
    ctx = lax.axis_size("ctx")
    place = lax.axis_index("ctx")
    first, last = place == 0, place == ctx - 1
    greet()
    swaps = exchange(part_ref, box, gsend, grecv)
    decay = decay_ref[:1, :]
    target = {"ctx": lax.rem(place + 1, ctx)}
    copies = []
    for k in range(inbox.shape[0]):
        copies.append(chain_step(k, first, last, target, inbox, outbox, send, recv, decay, state_ref))
        if k == 0:
            for swap in swaps:
                swap.start()
        sin_ref[CHUNK * k : CHUNK * (k + 1), :] = inbox[k]
    for swap in swaps:
        swap.wait()
    gu_ref[...] = gathered_sum(part_ref, box)

    @pl.when(jnp.logical_not(last))
    def _():
        for copy in copies:
            copy.wait_send()


def greet_all():
    ctx = lax.axis_size("ctx")
    place = lax.axis_index("ctx")
    barrier = pltpu.get_barrier_semaphore()
    peers = group_peers() + [{"ctx": lax.rem(place + d, ctx)} for d in range(1, ctx)]
    for peer in peers:
        pl.semaphore_signal(barrier, inc=1, device_id=peer, device_id_type=pl.DeviceIdType.MESH)
    pl.semaphore_wait(barrier, len(peers))


def middle_part(reduce_start, part_ref, up_ref, gout_ref, ginj_ref, decay_ref, gin_ref, out_ref,
                box, inbox, outbox, usend, urecv, send, recv):
    ctx = lax.axis_size("ctx")
    place = lax.axis_index("ctx")
    first, last = place == 0, place == ctx - 1
    chunks = inbox.shape[0]
    below = {"ctx": lax.rem(place + ctx - 1, ctx)}
    greet_all()
    swaps = exchange(part_ref, box, usend, urecv)
    copies = [remote(outbox.at[k], inbox.at[k], send.at[k], recv.at[k], below) for k in range(chunks)]

    def adapter():
        for swap in swaps:
            swap.wait()
        u = gathered_sum(part_ref, box)
        out_ref[...] = tn(u, up_ref[...]).astype(bf16)
        reduce_start(nn(u, gout_ref[...]))

    @pl.when(last)
    def _():
        for k in range(chunks):
            outbox[k] = ginj_ref[CHUNK * k : CHUNK * (k + 1), :]
            copies[k].start()
        gin_ref[...] = jnp.zeros_like(gin_ref)

    for swap in swaps:
        swap.start()

    early = place * 2 < ctx

    @pl.when(early)
    def _():
        adapter()

    decay = decay_ref[:1, :]

    @pl.when(jnp.logical_not(last))
    def _():
        for k in range(chunks):
            copies[k].wait_recv()

            @pl.when(jnp.logical_not(first))
            def _():
                outbox[k] = decay * inbox[k] + ginj_ref[CHUNK * k : CHUNK * (k + 1), :]
                copies[k].start()

            gin_ref[CHUNK * k : CHUNK * (k + 1), :] = inbox[k]

    @pl.when(jnp.logical_not(early))
    def _():
        adapter()

    @pl.when(jnp.logical_not(first))
    def _():
        for k in range(chunks):
            copies[k].wait_send()


def backward_kernel(heads, x_ref, b_ref, c_ref, e_ref, einv_ref, dt_ref, rc_ref, rr_ref, em_ref,
                    skip_ref, rate_ref, gy_ref, gd_ref, sin_ref, pn_ref, k_ref, decay_ref, ddown_ref, part_ref, up_ref, gout_ref, ginj_ref,
                    dx_ref, db_ref, dc_ref, dstep_ref, gdown_ref, gup_ref, out_ref,
                    gin_ref, box, inbox, outbox, usend, urecv, chain_send, chain_recv, mine, arrived, totals, send, recv, back_send, back_recv):
    rows = x_ref.shape[0]
    groups = b_ref.shape[1] // STATE
    width = x_ref.shape[1] // groups
    per_group = heads // groups
    ctx = lax.axis_size("ctx")
    place = lax.axis_index("ctx")
    share = mine.shape[1]
    rank = ddown_ref.shape[0]
    others = [lax.rem(place + d, ctx) for d in range(1, ctx)]
    out_copies = [
        remote(mine.at[j], arrived.at[d], send.at[d], recv.at[d], {"ctx": j}) for d, j in enumerate(others)
    ]
    back_copies = [
        remote(totals.at[place], totals.at[place], back_send.at[d], back_recv.at[d], {"ctx": j})
        for d, j in enumerate(others)
    ]

    def reduce_start(dup):
        for j in range(ctx):
            lo = j * share
            mine[j] = ddown_ref[lo : lo + share, :] if lo < rank else dup[lo - rank : lo - rank + share, :]
        for copy in out_copies:
            copy.start()

    middle_part(reduce_start, part_ref, up_ref, gout_ref, ginj_ref, decay_ref, gin_ref, out_ref,
                box, inbox, outbox, usend, urecv, chain_send, chain_recv)
    total = mine[place]
    for d, copy in enumerate(out_copies):
        copy.wait()
        total = total + arrived[d]
    totals[place] = total
    for copy in back_copies:
        copy.start()
    mask = score_mask(rc_ref[:, :1], rr_ref[:1, :])
    fresh = rc_ref[:, :1] == 0
    ends = rc_ref[:, :1] == rc_ref[rows - 1 : rows, :1]
    f_cols = dt_ref[...] * einv_ref[...]
    net = -pn_ref[...]
    step = jnp.zeros(pn_ref.shape, f32)
    kk = k_ref[...]
    for g in range(groups):
        cols = slice(g * width, (g + 1) * width)
        narrow = slice(g * STATE, (g + 1) * STATE)
        x = x_ref[:, cols].astype(f32)
        fx = expand(f_cols, g, per_group, width)
        xd = (x * fx).astype(bf16)
        gd = gd_ref[:, cols]
        b = b_ref[:, narrow]
        c = c_ref[:, narrow]
        a = jnp.where(mask, nt(c, b), 0.0).astype(bf16)
        b_end = jnp.where(ends, b, 0.0).astype(bf16)
        em = em_ref[:1, cols]
        sin = sin_ref[:, cols]
        gin = gin_ref[:, cols]
        s = (em * sin).astype(bf16)
        ge = (em * gin).astype(bf16)
        v = tn(a, gd) + nn(b_end, ge)
        dx_ref[:, cols] = (fx * v + wide_row(skip_ref[...], g, per_group, width) * gy_ref[:, cols]).astype(bf16)
        pair = jnp.where(mask, nt(gd, xd), 0.0).astype(bf16)
        dc_ref[:, narrow] = (nn(pair, b) + jnp.where(fresh, nt(gd, s), 0.0)).astype(bf16)
        db_ref[:, narrow] = (tn(pair, c) + jnp.where(ends, nt(xd, ge), 0.0)).astype(bf16)
        net = net + headsum(xd.astype(f32) * v, g, per_group)
        step = step + headsum(x * v, g, per_group)
        through = decay_ref[:1, cols] * jnp.sum(sin * gin, axis=0, keepdims=True)
        kk = kk + headsum(jnp.broadcast_to(through, (8, width)), g, per_group)
    before = jnp.where(iota((rows, rows), 0) > iota((rows, rows), 1), 1.0, 0.0)
    glog = lax.dot_general(before, net, (((1,), (0,)), ((), ())), precision=highest, preferred_element_type=f32) + kk[:1]
    gdt = einv_ref[...] * step - padded(rate_ref[...]) * glog
    out = gdt * (1.0 - jnp.exp(-dt_ref[...]))
    dstep_ref[...] = out.T[: dstep_ref.shape[0], :]
    for copy in back_copies:
        copy.wait()
    gdown_ref[...] = jnp.concatenate([totals[j] for j in range(ctx // 2)], axis=0).T
    gup_ref[...] = jnp.concatenate([totals[j] for j in range(ctx // 2, ctx)], axis=0)


def call(kernel, name, outs, args, scratch=(), collective_id=None):
    params = {} if collective_id is None else dict(collective_id=collective_id, has_side_effects=True)
    whole = pl.BlockSpec(memory_space=pltpu.VMEM)
    return pl.pallas_call(
        kernel,
        name=name,
        out_shape=[jax.ShapeDtypeStruct(s, d) for s, d in outs],
        in_specs=[whole] * len(args),
        out_specs=[whole] * len(outs),
        scratch_shapes=list(scratch),
        compiler_params=pltpu.CompilerParams(vmem_limit_bytes=56 << 20, **params),
    )(*args)


def per_device(x, z, b, c, dtin, resets, rate, bias, skip, gain, down, up, gx, gout):
    rows, channels = x.shape
    heads = dtin.shape[0]
    rank = down.shape[1]
    peers = lax.axis_size("head") * lax.axis_size("fsdp") - 1
    chunks = STATE // CHUNK
    assert 2 * rank == STATE
    dma = pltpu.SemaphoreType.DMA
    slab = pltpu.VMEM((chunks, CHUNK, channels), f32)
    swap = pltpu.VMEM((peers, rank, rows), f32)
    skip_row = skip[None, :]
    gain_row = gain[None, :]
    rate_row = rate[None, :]
    down_rows = down.T
    e, einv, dt, rc, rr, em, decay, state = call(
        scan_kernel, "scan",
        [((rows, LANES), f32)] * 4 + [((8, rows), f32), ((8, channels), f32), ((8, channels), f32), ((STATE, channels), f32)],
        (x, b, dtin, bias[None, :], rate_row, resets[None, :]),
    )
    gu_part = nt(up, gout)
    gu, sin = call(
        start_kernel, "start", [((rank, rows), bf16), ((STATE, channels), f32)], (gu_part, state, decay),
        [swap, slab, slab, dma((peers,)), dma((peers,)), dma((chunks,)), dma((chunks,))], 1,
    )
    mixed, dz, gy, gd, ginj, pn, kk, ddown, u_part = call(
        lambda *r: forward_kernel(heads, *r), "forward",
        [((rows, channels), bf16), ((rows, channels), bf16), ((rows, channels), f32), ((rows, channels), bf16),
         ((STATE, channels), f32), ((rows, LANES), f32), ((8, LANES), f32),
         ((rank, channels), f32), ((rank, rows), f32)],
        (x, z, b, c, gx, e, einv, dt, rc, rr, em, skip_row, gain_row, down_rows, gu, sin),
    )
    ctx = lax.axis_size("ctx")
    share = STATE // ctx
    dx, db, dc, dstep, gdown, gup, adapter_output = call(
        lambda *r: backward_kernel(heads, *r), "backward",
        [((rows, channels), bf16), (b.shape, bf16), (c.shape, bf16), ((heads, rows), f32),
         ((channels, rank), f32), ((rank, channels), f32), ((rows, channels), bf16)],
        (x, b, c, e, einv, dt, rc, rr, em, skip_row, rate_row, gy, gd, sin, pn, kk, decay, ddown, u_part, up, gout, ginj),
        [pltpu.VMEM((STATE, channels), f32), swap, slab, slab] + [dma((peers,))] * 2 + [dma((chunks,))] * 2
        + [pltpu.VMEM((ctx, share, channels), f32), pltpu.VMEM((ctx - 1, share, channels), f32),
           pltpu.VMEM((ctx, share, channels), f32)] + [dma((ctx - 1,))] * 4, 3,
    )
    return mixed, adapter_output, dx, dz, db, dc, dstep, gdown, gup


def solution(mesh):
    wide = P(("parts", "ctx"), ("head", "fsdp"))
    steps = P(("head", "fsdp"), ("parts", "ctx"))
    over_heads = P(("head", "fsdp"))
    in_specs = (
        wide, wide, wide, wide, steps, P(("parts", "ctx")), over_heads, over_heads, over_heads, over_heads,
        P(("head", "fsdp"), None), P(None, ("head", "fsdp")), wide, wide,
    )
    out_specs = (
        wide, wide, wide, wide, wide, wide, steps, P(("parts", "head", "fsdp"), None), P("parts", ("head", "fsdp")),
    )
    return jax.shard_map(per_device, mesh=mesh, in_specs=in_specs, out_specs=out_specs, check_vma=False)
```
